32 devices in a mesh: group: 4 (over y, x), dev: 8 (over z, core).
Axes of the slice: x: 2, y: 2, z: 4, core: 2. Of those that a mesh axis runs over, the one named last changes fastest.
Arguments:
- q_compressed: bfloat16 [32, 1536], P('group'), may hold values from -6 to 6
- w_q_nope: bfloat16 [1536, 16384], P(None, 'dev'), may hold values from -0.15625 to 0.15625
- w_q_rope: bfloat16 [1536, 8192], P(None, 'dev'), may hold values from -0.15625 to 0.15625
- w_uk: bfloat16 [128, 128, 512], P('dev'), may hold values from -0.5 to 0.5
- w_uv: bfloat16 [128, 512, 128], P('dev'), may hold values from -0.25 to 0.25
- w_o: bfloat16 [16384, 7168], P('dev'), may hold values from -0.046875 to 0.046875
- kv_cache: bfloat16 [4, 8, 2, 2048, 576], P('group', 'dev'), may hold values from -320 to 320
- draft_kv: bfloat16 [32, 576], P('group'), may hold values from -18 to 18
- context_length: int32 [8], replicated, may hold values from 6145 to 24576
- slot_sequence: int32 [4, 8, 2], replicated, may hold values from -1 to 7, as said below
- slot_slab: int32 [4, 8, 2], replicated, may hold values from -1 to 11
Outputs:
- attn_output: float32 [32, 7168], P(('group', 'dev'))
The draws below stay inside these ranges and needn't reach their ends.
Inputs may be any that keep to these rules, and one draw needn't show every extreme that they name: For each sequence s, slabs 0 to ceil(context_length[s] / 2048) - 1 each stand in exactly one slot of the pool, slot_sequence naming s and slot_slab the slab's number; all other slots hold -1 in both tables. The sequences' slab counts are, in some order, 4 + floor(i * 8 / 7) for i from 0 to 7. A group's slots take the slabs of its own sequences first; slabs beyond a group's 8 * 2 slots stand in free slots of other groups.
All inputs are finite; a program needn't handle non-finite values.
Results may differ from the reference program's by a relative error of at most 0.02.
The reference program's roundings to bfloat16 on the way (of `q_nope`, `queries`, `attended` and `head_values`) count: a program that leaves them out, or rounds other values in their place, can miss the bound.
Values may be sent and summed in bfloat16 or wider, within the bound.
A program may use at most 128 MiB of HBM per device.

```python
import jax
import jax.numpy as jnp
from jax import lax

D = 7168
HEADS = 128
QRANK = 1536
NOPE = 128
ROPE = 64
LATENT = 512
VDIM = 128
DRAFT = 4
SLOTS = 2
MIN_SLABS = 4
MAX_SLABS = 12
SLAB = 2048
GROUPS = 4
HOLDERS = 8
SEQ_GRP = 2
SEQS = 8
TOKENS = 32
KV = 576


def placement(key):
    base_key = jax.random.fold_in(key, 5)
    key_heavy, key_order, key_tail, key_spread = jax.random.split(base_key, 4)
    seq_count = SEQ_GRP * GROUPS
    capacity = HOLDERS * SLOTS
    heavy = jax.random.randint(key_heavy, (), 0, GROUPS)
    home_group = jnp.arange(seq_count, dtype=jnp.int32) // SEQ_GRP
    score = jnp.where(home_group == heavy, seq_count, 0) + jax.random.permutation(key_order, seq_count).astype(jnp.int32)
    ranking = jnp.argsort(jnp.argsort(score, stable=True), stable=True).astype(jnp.int32)
    slab_count = MIN_SLABS + ranking * (MAX_SLABS - MIN_SLABS) // (seq_count - 1)
    tail_tokens = jax.random.randint(key_tail, (seq_count,), 1, SLAB + 1)
    tail_tokens = jnp.where(ranking == 0, 1, jnp.where(ranking == seq_count - 1, SLAB, tail_tokens))
    lengths = ((slab_count - 1) * SLAB + tail_tokens).astype(jnp.int32)
    per_group = slab_count.reshape(GROUPS, SEQ_GRP)
    starts = jnp.cumsum(per_group, axis=1) - per_group
    load = jnp.sum(per_group, axis=1)
    kept = jnp.minimum(load, capacity)
    spill = load - kept
    free_slots = capacity - kept
    spill_start = jnp.cumsum(spill) - spill
    free_start = jnp.cumsum(free_slots) - free_slots
    position = jnp.arange(capacity, dtype=jnp.int32)
    at_home = position[None, :] < kept[:, None]
    free_rank = free_start[:, None] + position[None, :] - kept[:, None]
    used_spill = jnp.logical_not(at_home) & (free_rank < jnp.sum(spill))
    inside = (spill_start[None, None, :] <= free_rank[:, :, None]) & (free_rank[:, :, None] < (spill_start + spill)[None, None, :])
    source = jnp.sum(inside.astype(jnp.int32) * jnp.arange(GROUPS, dtype=jnp.int32)[None, None, :], axis=2)
    owner_group = jnp.where(at_home, jnp.arange(GROUPS, dtype=jnp.int32)[:, None], source)
    group_rank = jnp.where(at_home, position[None, :], capacity + free_rank - spill_start[source])
    owner_starts = starts[owner_group]
    member = jnp.sum((owner_starts <= group_rank[:, :, None]).astype(jnp.int32), axis=2) - 1
    member = jnp.clip(member, 0, SEQ_GRP - 1)
    sequence = owner_group * SEQ_GRP + member
    slab_number = group_rank - jnp.take_along_axis(owner_starts, member[..., None], axis=2)[..., 0]
    live = at_home | used_spill
    sequence = jnp.where(live, sequence, -1)
    slab_number = jnp.where(live, slab_number, -1)
    perms = jnp.stack([jax.random.permutation(jax.random.fold_in(key_spread, group_id), HOLDERS) for group_id in range(GROUPS)])
    inverse = jnp.argsort(perms, axis=1).astype(jnp.int32)
    spot = jnp.arange(SLOTS, dtype=jnp.int32)[None, None, :] * HOLDERS + inverse[:, :, None]
    spot = spot.reshape(GROUPS, -1)
    table_sequence = jnp.take_along_axis(sequence, spot, axis=1).reshape(GROUPS, HOLDERS, SLOTS)
    table_slab = jnp.take_along_axis(slab_number, spot, axis=1).reshape(GROUPS, HOLDERS, SLOTS)
    return (lengths, table_sequence.astype(jnp.int32), table_slab.astype(jnp.int32))


def draw_context_length(key, part):
    return placement(key)[0]


def draw_slot_sequence(key, part):
    return placement(key)[1]


def draw_slot_slab(key, part):
    return placement(key)[2]


def draw_kv_cache(key, part):
    shape = (GROUPS, HOLDERS, SLOTS, SLAB, LATENT + ROPE)
    key_base = jax.random.fold_in(jax.random.fold_in(key, 11), 0)
    drawn = jnp.clip(1.5 * jax.random.normal(key_base, shape, jnp.float32), -9.0, 9.0)
    return drawn.astype(jnp.bfloat16)


def block_levels(key, shape, shards, smallest, largest):
    gain, own = 1.0, jax.random.fold_in(key, 6)
    for axis_at, blocks in shards:
        heights = jnp.exp(jax.random.uniform(jax.random.fold_in(own, axis_at), (blocks,), jnp.float32, smallest / len(shards), largest / len(shards)))
        gain = gain * jnp.repeat(heights, shape[axis_at] // blocks).reshape([-1 if axis == axis_at else 1 for axis in range(len(shape))])
    return gain


def noise(rng, extent, spread, limit, cuts=(), held_as=jnp.bfloat16):
    result = jax.random.normal(rng, extent, jnp.float32) * spread
    if len(cuts) > 0:
        result = block_levels(rng, extent, cuts, -0.22, 0.18) * result
    return jnp.clip(result, min=-limit, max=limit).astype(held_as)


def setup_inputs(seed: int = 0) -> dict:
    keys = jax.random.split(jax.random.key(seed), 12)
    return {
        "q_compressed": noise(keys[0], (TOKENS, QRANK), 1.0, 6.0, ((0, 4),)),
        "w_q_nope": noise(keys[1], (QRANK, HEADS * NOPE), QRANK ** -0.5, 0.15625, ((1, 8),)),
        "w_q_rope": noise(keys[2], (QRANK, HEADS * ROPE), QRANK ** -0.5, 0.15625, ((1, 8),)),
        "w_uk": noise(keys[3], (HEADS, NOPE, LATENT), NOPE ** -0.5, 0.5, ((0, 8),)),
        "w_uv": noise(keys[4], (HEADS, LATENT, VDIM), LATENT ** -0.5, 0.25, ((0, 8),)),
        "w_o": noise(keys[5], (HEADS * VDIM, D), (HEADS * VDIM) ** -0.5, 0.046875, ((0, 8),)),
        "kv_cache": draw_kv_cache(jax.random.fold_in(keys[11], 71), 0),
        "draft_kv": noise(keys[7], (TOKENS, KV), 3.0, 18.0, ((0, 4),)),
        "context_length": draw_context_length(jax.random.fold_in(keys[11], 71), 0),
        "slot_sequence": draw_slot_sequence(jax.random.fold_in(keys[11], 71), 0),
        "slot_slab": draw_slot_slab(jax.random.fold_in(keys[11], 71), 0),
    }


EMPTY = -1e30


def slot_partial(row_block, slab_keys, valid_count):
    scores = lax.dot_general(row_block, slab_keys, (((1,), (1,)), ((), ())), preferred_element_type=jnp.float32)
    is_valid = jnp.arange(slab_keys.shape[0], dtype=jnp.int32) < valid_count
    masked = jnp.where(is_valid[None, :], scores, EMPTY)
    row_peak = jnp.max(masked, axis=1)
    weights = jnp.where(is_valid[None, :], jnp.exp(masked - row_peak[:, None]), 0.0)
    row_total = jnp.maximum(jnp.sum(weights, axis=1), 1.0)
    mixture = jnp.dot(weights.astype(jnp.bfloat16), slab_keys[:, :LATENT], preferred_element_type=jnp.float32)
    return row_peak + jnp.log(row_total), mixture / row_total[:, None]


def merge_blocks(block_log, block_out, block_owner, own_log, own_out):
    owners_count = own_log.shape[0]
    matches = block_owner[None, :] == jnp.arange(owners_count, dtype=jnp.int32)[:, None]
    picked = jnp.where(matches[:, :, None, None], block_log[None], EMPTY)
    top_log = jnp.maximum(jnp.max(picked, axis=1), own_log)
    weights = jnp.where(matches[:, :, None, None], jnp.exp(picked - top_log[:, None]), 0.0)
    own_weight = jnp.exp(own_log - top_log)
    weight_sum = jnp.sum(weights, axis=1) + own_weight
    summed = jnp.einsum('sbtx,btxl->stxl', weights, block_out, precision=lax.Precision.HIGHEST)
    summed = summed + own_weight[..., None] * own_out
    return top_log + jnp.log(weight_sum), summed / weight_sum[..., None]


def reference(q_compressed, w_q_nope, w_q_rope, w_uk, w_uv, w_o, kv_cache, draft_kv, context_length, slot_sequence, slot_slab):
    token_count = q_compressed.shape[0]
    key_width = LATENT + ROPE
    q_nope = jnp.dot(q_compressed, w_q_nope, preferred_element_type=jnp.float32).astype(jnp.bfloat16)
    q_nope = q_nope.reshape(token_count, HEADS, NOPE)
    q_rope = jnp.dot(q_compressed, w_q_rope, preferred_element_type=jnp.float32).reshape(token_count, HEADS, ROPE)
    absorbed = jnp.einsum('thn,hnl->thl', q_nope.astype(jnp.float32), w_uk.astype(jnp.float32), precision=lax.Precision.HIGHEST)
    queries = (jnp.concatenate([absorbed, q_rope], axis=2) * (NOPE + ROPE) ** -0.5).astype(jnp.bfloat16)
    by_sequence = queries.reshape(SEQS, DRAFT * HEADS, key_width)
    pool_owner = slot_sequence.reshape(-1).astype(jnp.int32)
    pool_number = slot_slab.reshape(-1).astype(jnp.int32)
    slabs_flat = kv_cache.reshape(-1, SLAB, key_width)

    def one_slot(slot_number):
        slot_owner = pool_owner[slot_number]
        chosen = jnp.maximum(slot_owner, 0)
        row_block = lax.dynamic_index_in_dim(by_sequence, chosen, 0, keepdims=False)
        valid_count = jnp.where(slot_owner >= 0, context_length[chosen] - pool_number[slot_number] * SLAB, 0)
        slab_keys = lax.dynamic_index_in_dim(slabs_flat, slot_number, 0, keepdims=False)
        return slot_partial(row_block, slab_keys, valid_count)

    slot_log, slot_out = lax.map(one_slot, jnp.arange(pool_owner.shape[0], dtype=jnp.int32))
    slot_log = slot_log.reshape(-1, DRAFT, HEADS)
    slot_out = slot_out.reshape(-1, DRAFT, HEADS, LATENT)

    draft_rows = queries.reshape(SEQS, DRAFT, HEADS, key_width).astype(jnp.float32)
    draft_keys = draft_kv.reshape(SEQS, DRAFT, key_width).astype(jnp.float32)
    scores = jnp.einsum('sthk,suk->sthu', draft_rows, draft_keys, precision=lax.Precision.HIGHEST)
    causal = jnp.arange(DRAFT)[None, :] <= jnp.arange(DRAFT)[:, None]
    masked = jnp.where(causal[None, :, None, :], scores, EMPTY)
    draft_peak = jnp.max(masked, axis=3)
    weights = jnp.where(causal[None, :, None, :], jnp.exp(masked - draft_peak[..., None]), 0.0)
    draft_total = jnp.sum(weights, axis=3)
    rounded = lax.optimization_barrier(weights.astype(jnp.bfloat16)).astype(jnp.float32)
    mixture = jnp.einsum('sthu,sul->sthl', rounded, draft_keys[..., :LATENT], precision=lax.Precision.HIGHEST)
    draft_log = draft_peak + jnp.log(draft_total)
    draft_out = mixture / draft_total[..., None]

    final_log, final_out = merge_blocks(slot_log, slot_out, pool_owner, draft_log, draft_out)
    attended = final_out.astype(jnp.bfloat16).reshape(token_count, HEADS, LATENT)
    head_values = jnp.einsum('thl,hlv->thv', attended.astype(jnp.float32), w_uv.astype(jnp.float32), precision=lax.Precision.HIGHEST)
    head_values = head_values.astype(jnp.bfloat16).reshape(token_count, HEADS * VDIM)
    return jnp.dot(head_values, w_o, preferred_element_type=jnp.float32)
```

```python
import jax
import jax.numpy as jnp
from jax import lax
from jax.experimental import pallas as pl
from jax.experimental.pallas import tpu as pltpu
from jax.sharding import PartitionSpec as P

NOPE = 128
ROPE = 64
LATENT = 512
VDIM = 128
DRAFT = 4


EMPTY = -1e30


def exchange(axis, call_id, *blocks):
    count = lax.axis_size(axis)
    number = len(blocks)

    def body(*refs):
        sent, got = refs[:number], refs[number : 2 * number]
        send_sems, recv_sems, local_sems = refs[2 * number :]
        me = lax.axis_index(axis)
        barrier = pltpu.get_barrier_semaphore()
        for step in range(1, count):
            pl.semaphore_signal(
                barrier,
                inc=1,
                device_id={axis: lax.rem(me + step, count)},
                device_id_type=pl.DeviceIdType.MESH,
            )
        pl.semaphore_wait(barrier, count - 1)
        started = []
        for step in range(1, count):
            peer = lax.rem(me + step, count)
            for which in range(number):
                copy = pltpu.make_async_remote_copy(
                    src_ref=sent[which].at[peer],
                    dst_ref=got[which].at[me],
                    send_sem=send_sems.at[which, step],
                    recv_sem=recv_sems.at[which, step],
                    device_id={axis: peer},
                    device_id_type=pl.DeviceIdType.MESH,
                )
                copy.start()
                started.append(copy)
        own = []
        for which in range(number):
            copy = pltpu.make_async_copy(
                sent[which].at[me], got[which].at[me], local_sems.at[which]
            )
            copy.start()
            own.append(copy)
        for copy in own:
            copy.wait()
        for copy in started:
            copy.wait()

    vmem = pl.BlockSpec(memory_space=pltpu.VMEM)
    return pl.pallas_call(
        body,
        out_shape=tuple(jax.ShapeDtypeStruct(block.shape, block.dtype) for block in blocks),
        in_specs=[vmem] * number,
        out_specs=tuple([vmem] * number),
        scratch_shapes=[
            pltpu.SemaphoreType.DMA((number, count)),
            pltpu.SemaphoreType.DMA((number, count)),
            pltpu.SemaphoreType.DMA((number,)),
        ],
        compiler_params=pltpu.CompilerParams(
            collective_id=call_id, has_side_effects=True, vmem_limit_bytes=32 * 1024 * 1024
        ),
        name="exchange_%d" % call_id,
    )(*blocks)


def exchange_partials(axis, call_id, block_log, block_mix):
    count = lax.axis_size(axis)
    flat_log = block_log.reshape(count, 1, -1)
    width = flat_log.shape[2]
    padded = -(-width // 128) * 128
    flat_log = jnp.pad(flat_log, ((0, 0), (0, 0), (0, padded - width)))
    flat_mix = block_mix.astype(jnp.bfloat16).reshape(count, -1, block_mix.shape[-1])
    got_log, got_mix = exchange(axis, call_id, flat_log, flat_mix)
    return (
        got_log[:, :, :width].reshape(block_log.shape),
        got_mix.reshape(block_mix.shape).astype(jnp.float32),
    )


def slot_partial(row_block, slab_keys, valid_count):
    scores = lax.dot_general(
        row_block, slab_keys, (((1,), (1,)), ((), ())), preferred_element_type=jnp.float32
    )
    is_valid = jnp.arange(slab_keys.shape[0], dtype=jnp.int32) < valid_count
    masked = jnp.where(is_valid[None, :], scores, EMPTY)
    row_peak = jnp.max(masked, axis=1)
    weights = jnp.where(is_valid[None, :], jnp.exp(masked - row_peak[:, None]), 0.0)
    row_total = jnp.maximum(jnp.sum(weights, axis=1), 1.0)
    mixture = jnp.dot(
        weights.astype(jnp.bfloat16), slab_keys[:, :LATENT], preferred_element_type=jnp.float32
    )
    return (row_peak + jnp.log(row_total), mixture / row_total[:, None])


def merge_blocks(block_log, block_out, block_owner, own_log, own_out):
    owners_count = own_log.shape[0]
    matches = block_owner[None, :] == jnp.arange(owners_count, dtype=jnp.int32)[:, None]
    picked = jnp.where(matches[:, :, None, None], block_log[None], EMPTY)
    top_log = jnp.maximum(jnp.max(picked, axis=1), own_log)
    weights = jnp.where(matches[:, :, None, None], jnp.exp(picked - top_log[:, None]), 0.0)
    own_weight = jnp.exp(own_log - top_log)
    weight_sum = jnp.sum(weights, axis=1) + own_weight
    summed = jnp.einsum("sbtx,btxl->stxl", weights, block_out, precision=lax.Precision.HIGHEST)
    summed = summed + own_weight[..., None] * own_out
    return (top_log + jnp.log(weight_sum), summed / weight_sum[..., None])


def draft_partials(queries_seq, draft_rows):
    scores = jnp.einsum(
        "sthk,suk->sthu", queries_seq, draft_rows, preferred_element_type=jnp.float32
    )
    causal = jnp.arange(DRAFT)[None, :] <= jnp.arange(DRAFT)[:, None]
    masked = jnp.where(causal[None, :, None, :], scores, EMPTY)
    draft_peak = jnp.max(masked, axis=3)
    weights = jnp.where(causal[None, :, None, :], jnp.exp(masked - draft_peak[..., None]), 0.0)
    draft_total = jnp.sum(weights, axis=3)
    mixture = jnp.einsum(
        "sthu,sul->sthl",
        weights.astype(jnp.bfloat16),
        draft_rows[..., :LATENT],
        preferred_element_type=jnp.float32,
    )
    return (draft_peak + jnp.log(draft_total), mixture / draft_total[..., None])


def holder_partials(arrived, cache_slots, valid_counts):
    holder_count, slot_count, draft_count, heads_here, key_width = arrived.shape
    log_list = []
    mix_list = []
    for slot_id in range(slot_count):
        row_block = arrived[:, slot_id].reshape(holder_count * draft_count * heads_here, key_width)
        slot_log, slot_mix = slot_partial(row_block, cache_slots[slot_id], valid_counts[slot_id])
        log_list.append(slot_log.reshape(holder_count, draft_count, heads_here))
        mix_list.append(slot_mix.reshape(holder_count, draft_count, heads_here, LATENT))
    return (jnp.stack(log_list, axis=1), jnp.stack(mix_list, axis=1))


def shards(
    q_compressed,
    w_q_nope,
    w_q_rope,
    w_uk,
    w_uv,
    w_o,
    kv_cache,
    draft_kv,
    context_length,
    slot_sequence,
    slot_slab,
):
    group_count = lax.axis_size("group")
    holder_count = lax.axis_size("dev")
    group_index = lax.axis_index("group")
    holder_index = lax.axis_index("dev")
    token_count = q_compressed.shape[0]
    seq_group = token_count // DRAFT
    heads_here = w_uk.shape[0]
    key_width = LATENT + ROPE
    slab_length = kv_cache.shape[3]
    q_nope = jnp.dot(q_compressed, w_q_nope, preferred_element_type=jnp.float32).astype(
        jnp.bfloat16
    )
    q_nope = q_nope.reshape(token_count, heads_here, NOPE)
    q_rope = jnp.dot(q_compressed, w_q_rope, preferred_element_type=jnp.float32).reshape(
        token_count, heads_here, ROPE
    )
    absorbed = jnp.einsum("thn,hnl->thl", q_nope, w_uk, preferred_element_type=jnp.float32)
    queries = (jnp.concatenate([absorbed, q_rope], axis=2) * (NOPE + ROPE) ** (-0.5)).astype(
        jnp.bfloat16
    )
    queries_seq = queries.reshape(seq_group, DRAFT, heads_here, key_width)
    draft_log, draft_mix = draft_partials(
        queries_seq, draft_kv.reshape(seq_group, DRAFT, key_width)
    )
    group_table = lax.dynamic_index_in_dim(slot_sequence, group_index, 0, keepdims=False)
    own_table = lax.dynamic_index_in_dim(group_table, holder_index, 0, keepdims=False)
    own_slabs = lax.dynamic_index_in_dim(
        lax.dynamic_index_in_dim(slot_slab, group_index, 0, keepdims=False),
        holder_index,
        0,
        keepdims=False,
    )
    chosen = jnp.maximum(own_table, 0)
    valid_counts = jnp.where(own_table >= 0, context_length[chosen] - own_slabs * slab_length, 0)
    cache_slots = kv_cache[0, 0]
    outgoing = jnp.broadcast_to(
        queries_seq.reshape(1, -1, key_width), (group_count, token_count * heads_here, key_width)
    )
    (gathered,) = exchange("group", 0, outgoing)
    every_seq = gathered.reshape(group_count * seq_group, DRAFT, heads_here, key_width)
    picked = jnp.take(every_seq, jnp.maximum(group_table, 0).reshape(-1), axis=0)
    (arrived,) = exchange("dev", 1, picked.reshape(holder_count, -1, key_width))
    arrived = arrived.reshape(holder_count, -1, DRAFT, heads_here, key_width)
    slot_log, slot_mix = holder_partials(arrived, cache_slots, valid_counts)
    back_log, back_mix = exchange_partials("dev", 2, slot_log, slot_mix)
    seq_total = group_count * seq_group
    group_log, group_mix = merge_blocks(
        back_log.reshape(-1, DRAFT, heads_here),
        back_mix.reshape(-1, DRAFT, heads_here, LATENT),
        group_table.reshape(-1),
        jnp.full((seq_total, DRAFT, heads_here), EMPTY, jnp.float32),
        jnp.zeros((seq_total, DRAFT, heads_here, LATENT), jnp.float32),
    )
    home_log, home_mix = exchange_partials(
        "group",
        3,
        group_log.reshape(group_count, seq_group, DRAFT, heads_here),
        group_mix.reshape(group_count, seq_group, DRAFT, heads_here, LATENT),
    )
    home_owner = jnp.tile(jnp.arange(seq_group, dtype=jnp.int32), group_count)
    final_log, final_mix = merge_blocks(
        home_log.reshape(-1, DRAFT, heads_here),
        home_mix.reshape(-1, DRAFT, heads_here, LATENT),
        home_owner,
        draft_log,
        draft_mix,
    )
    attended = final_mix.astype(jnp.bfloat16).reshape(token_count, heads_here, LATENT)
    head_values = jnp.einsum("thl,hlv->thv", attended, w_uv, preferred_element_type=jnp.float32)
    head_values = head_values.astype(jnp.bfloat16).reshape(token_count, heads_here * VDIM)
    partial = jnp.dot(head_values, w_o, preferred_element_type=jnp.float32)
    (terms,) = exchange(
        "dev", 4, partial.reshape(holder_count, token_count // holder_count, -1)
    )
    return jnp.sum(terms, axis=0)


def solution(mesh):
    placed = (
        P("group", None),
        P(None, "dev"),
        P(None, "dev"),
        P("dev", None, None),
        P("dev", None, None),
        P("dev", None),
        P("group", "dev", None, None, None),
        P("group", None),
        P(),
        P(),
        P(),
    )
    return jax.shard_map(
        shards, mesh=mesh, in_specs=placed, out_specs=P(("group", "dev"), None), check_vma=False
    )
```

```python
import jax
import jax.numpy as jnp
from jax import lax
from jax.experimental import pallas as pl
from jax.experimental.pallas import tpu as pltpu
from jax.sharding import PartitionSpec as P

NOPE = 128
ROPE = 64
LATENT = 512
VDIM = 128
DRAFT = 4


EMPTY = -1e30


def exchange(axis, call_id, *blocks):
    count = lax.axis_size(axis)
    number = len(blocks)

    def body(*refs):
        sent, got = refs[:number], refs[number : 2 * number]
        send_sems, recv_sems, local_sems = refs[2 * number :]
        me = lax.axis_index(axis)
        barrier = pltpu.get_barrier_semaphore()
        for step in range(1, count):
            pl.semaphore_signal(
                barrier,
                inc=1,
                device_id={axis: lax.rem(me + step, count)},
                device_id_type=pl.DeviceIdType.MESH,
            )
        pl.semaphore_wait(barrier, count - 1)
        started = []
        for step in range(1, count):
            peer = lax.rem(me + step, count)
            for which in range(number):
                copy = pltpu.make_async_remote_copy(
                    src_ref=sent[which].at[peer],
                    dst_ref=got[which].at[me],
                    send_sem=send_sems.at[which, step],
                    recv_sem=recv_sems.at[which, step],
                    device_id={axis: peer},
                    device_id_type=pl.DeviceIdType.MESH,
                )
                copy.start()
                started.append(copy)
        own = []
        for which in range(number):
            copy = pltpu.make_async_copy(
                sent[which].at[me], got[which].at[me], local_sems.at[which]
            )
            copy.start()
            own.append(copy)
        for copy in own:
            copy.wait()
        for copy in started:
            copy.wait()

    vmem = pl.BlockSpec(memory_space=pltpu.VMEM)
    return pl.pallas_call(
        body,
        out_shape=tuple(jax.ShapeDtypeStruct(block.shape, block.dtype) for block in blocks),
        in_specs=[vmem] * number,
        out_specs=tuple([vmem] * number),
        scratch_shapes=[
            pltpu.SemaphoreType.DMA((number, count)),
            pltpu.SemaphoreType.DMA((number, count)),
            pltpu.SemaphoreType.DMA((number,)),
        ],
        compiler_params=pltpu.CompilerParams(
            collective_id=call_id, has_side_effects=True, vmem_limit_bytes=8 * 1024 * 1024
        ),
        name="exchange_%d" % call_id,
    )(*blocks)


def exchange_partials(axis, call_id, block_log, block_mix):
    count = lax.axis_size(axis)
    flat_log = block_log.reshape(count, 1, -1)
    width = flat_log.shape[2]
    padded = -(-width // 128) * 128
    flat_log = jnp.pad(flat_log, ((0, 0), (0, 0), (0, padded - width)))
    flat_mix = block_mix.astype(jnp.bfloat16).reshape(count, -1, block_mix.shape[-1])
    got_log, got_mix = exchange(axis, call_id, flat_log, flat_mix)
    return (
        got_log[:, :, :width].reshape(block_log.shape),
        got_mix.reshape(block_mix.shape).astype(jnp.float32),
    )


def attend_slots(call_id, every_seq, cache_slots, context_length, slot_sequence, slot_slab):
    count = lax.axis_size("dev")
    slot_count, slab_length, key_width = cache_slots.shape
    seq_total, rows, _ = every_seq.shape
    chunk = min(count, max(1, 128 // rows))
    while count % chunk:
        chunk -= 1
    steps = count // chunk
    lanes = -(-rows // 128) * 128
    log_rows = -(-slot_count // 8) * 8

    def body(
        lengths, owners, slabs, every, cache, got_log, got_mix,
        staged, arrived, keys, log_stage, mix_stage,
        key_sems, send_sems, arrive_sems, back_send, back_recv,
    ):
        group = lax.axis_index("group")
        me = lax.axis_index("dev")
        barrier = pltpu.get_barrier_semaphore()

        def greet(step, carry):
            pl.semaphore_signal(
                barrier,
                inc=1,
                device_id={"dev": lax.rem(me + step, count)},
                device_id_type=pl.DeviceIdType.MESH,
            )
            return carry

        lax.fori_loop(1, count, greet, 0)
        for slot in range(slot_count):
            pltpu.make_async_copy(cache.at[slot], keys.at[slot], key_sems.at[slot]).start()
        pl.semaphore_wait(barrier, count - 1)

        def row_copy(peer, source):
            return pltpu.make_async_remote_copy(
                src_ref=staged.at[peer],
                dst_ref=arrived.at[source],
                send_sem=send_sems.at[peer],
                recv_sem=arrive_sems.at[source],
                device_id={"dev": peer},
                device_id_type=pl.DeviceIdType.MESH,
            )

        def back_copies(peer, source):
            return [
                pltpu.make_async_remote_copy(
                    src_ref=stage.at[peer],
                    dst_ref=target.at[source],
                    send_sem=back_send.at[which, peer],
                    recv_sem=back_recv.at[which, source],
                    device_id={"dev": peer},
                    device_id_type=pl.DeviceIdType.MESH,
                )
                for which, (stage, target) in enumerate([(log_stage, got_log), (mix_stage, got_mix)])
            ]

        def send_rows(step, carry):
            peer = lax.rem(me + step, count)
            for slot in range(slot_count):
                owner = jnp.maximum(owners[group, peer * slot_count + slot], 0)
                staged[peer, slot] = every[owner]
            row_copy(peer, me).start()
            return carry

        lax.fori_loop(1, count, send_rows, 0)
        limits = []
        for slot in range(slot_count):
            owner = owners[group, me * slot_count + slot]
            arrived[me, slot] = every[jnp.maximum(owner, 0)]
            left = lengths[jnp.maximum(owner, 0)] - slabs[group, me * slot_count + slot] * slab_length
            limits.append(jnp.where(owner >= 0, left, 0))
        for slot in range(slot_count):
            pltpu.make_async_copy(cache.at[slot], keys.at[slot], key_sems.at[slot]).wait()

        def one_step(step, carry):
            first = lax.rem(me // chunk + steps - step, steps) * chunk
            for at in range(chunk):
                source = first + at

                @pl.when(source != me)
                def _():
                    row_copy(source, source).wait_recv()

            for slot in range(slot_count):
                block = arrived[pl.ds(first, chunk), slot].reshape(chunk * rows, key_width)
                scores = lax.dot_general(
                    block, keys[slot], (((1,), (1,)), ((), ())), preferred_element_type=jnp.float32
                )
                place = lax.broadcasted_iota(jnp.int32, (1, slab_length), 1)
                is_valid = place < limits[slot]
                masked = jnp.where(is_valid, scores, EMPTY)
                peak = jnp.max(masked, axis=1, keepdims=True)
                weights = jnp.where(is_valid, jnp.exp(masked - peak), 0.0)
                total = jnp.maximum(jnp.sum(weights, axis=1, keepdims=True), 1.0)
                mixture = jnp.dot(
                    weights.astype(jnp.bfloat16),
                    keys[slot, :, :LATENT],
                    preferred_element_type=jnp.float32,
                )
                log = jnp.broadcast_to(peak + jnp.log(total), (chunk * rows, 128))
                mix = (mixture / total).astype(jnp.bfloat16).reshape(chunk, rows, LATENT)
                for at in range(chunk):
                    mix_stage[first + at, slot] = mix[at]
                    turned = jnp.transpose(log[at * rows : (at + 1) * rows])
                    log_stage[first + at, slot : slot + 1, :rows] = turned[:1]
            for at in range(chunk):
                source = first + at

                @pl.when(source != me)
                def _():
                    for copy in back_copies(source, me):
                        copy.start()

            return carry

        lax.fori_loop(0, steps, one_step, 0)
        got_log[me] = log_stage[me]
        got_mix[me] = mix_stage[me]

        def finish(step, carry):
            peer = lax.rem(me + step, count)
            row_copy(peer, peer).wait_send()
            for copy in back_copies(peer, peer):
                copy.wait_send()
                copy.wait_recv()
            return carry

        lax.fori_loop(1, count, finish, 0)

    smem = pl.BlockSpec(memory_space=pltpu.SMEM)
    vmem = pl.BlockSpec(memory_space=pltpu.VMEM)
    log_shape = (count, log_rows, lanes)
    mix_shape = (count, slot_count, rows, LATENT)
    group_count = slot_sequence.shape[0]
    got_log, got_mix = pl.pallas_call(
        body,
        out_shape=(
            jax.ShapeDtypeStruct(log_shape, jnp.float32),
            jax.ShapeDtypeStruct(mix_shape, jnp.bfloat16),
        ),
        in_specs=[smem, smem, smem, vmem, pl.BlockSpec(memory_space=pl.ANY)],
        out_specs=(vmem, vmem),
        scratch_shapes=[
            pltpu.VMEM((count, slot_count, rows, key_width), jnp.bfloat16),
            pltpu.VMEM((count, slot_count, rows, key_width), jnp.bfloat16),
            pltpu.VMEM((slot_count, slab_length, key_width), jnp.bfloat16),
            pltpu.VMEM(log_shape, jnp.float32),
            pltpu.VMEM(mix_shape, jnp.bfloat16),
            pltpu.SemaphoreType.DMA((slot_count,)),
            pltpu.SemaphoreType.DMA((count,)),
            pltpu.SemaphoreType.DMA((count,)),
            pltpu.SemaphoreType.DMA((2, count)),
            pltpu.SemaphoreType.DMA((2, count)),
        ],
        compiler_params=pltpu.CompilerParams(
            collective_id=call_id, has_side_effects=True, vmem_limit_bytes=24 * 1024 * 1024
        ),
        name="attend_slots",
    )(
        context_length,
        slot_sequence.reshape(group_count, -1),
        slot_slab.reshape(group_count, -1),
        every_seq,
        cache_slots,
    )
    return got_log[:, :slot_count, :rows], got_mix.astype(jnp.float32)


def merge_blocks(block_log, block_out, block_owner, own_log, own_out):
    owners_count = own_log.shape[0]
    matches = block_owner[None, :] == jnp.arange(owners_count, dtype=jnp.int32)[:, None]
    picked = jnp.where(matches[:, :, None, None], block_log[None], EMPTY)
    top_log = jnp.maximum(jnp.max(picked, axis=1), own_log)
    weights = jnp.where(matches[:, :, None, None], jnp.exp(picked - top_log[:, None]), 0.0)
    own_weight = jnp.exp(own_log - top_log)
    weight_sum = jnp.sum(weights, axis=1) + own_weight
    summed = jnp.einsum("sbtx,btxl->stxl", weights, block_out, precision=lax.Precision.HIGHEST)
    summed = summed + own_weight[..., None] * own_out
    return (top_log + jnp.log(weight_sum), summed / weight_sum[..., None])


def draft_partials(queries_seq, draft_rows):
    scores = jnp.einsum(
        "sthk,suk->sthu", queries_seq, draft_rows, preferred_element_type=jnp.float32
    )
    causal = jnp.arange(DRAFT)[None, :] <= jnp.arange(DRAFT)[:, None]
    masked = jnp.where(causal[None, :, None, :], scores, EMPTY)
    draft_peak = jnp.max(masked, axis=3)
    weights = jnp.where(causal[None, :, None, :], jnp.exp(masked - draft_peak[..., None]), 0.0)
    draft_total = jnp.sum(weights, axis=3)
    mixture = jnp.einsum(
        "sthu,sul->sthl",
        weights.astype(jnp.bfloat16),
        draft_rows[..., :LATENT],
        preferred_element_type=jnp.float32,
    )
    return (draft_peak + jnp.log(draft_total), mixture / draft_total[..., None])


def shards(
    q_compressed,
    w_q_nope,
    w_q_rope,
    w_uk,
    w_uv,
    w_o,
    kv_cache,
    draft_kv,
    context_length,
    slot_sequence,
    slot_slab,
):
    group_count = lax.axis_size("group")
    holder_count = lax.axis_size("dev")
    group_index = lax.axis_index("group")
    token_count = q_compressed.shape[0]
    seq_group = token_count // DRAFT
    heads_here = w_uk.shape[0]
    key_width = LATENT + ROPE
    q_nope = jnp.dot(q_compressed, w_q_nope, preferred_element_type=jnp.float32).astype(
        jnp.bfloat16
    )
    q_nope = q_nope.reshape(token_count, heads_here, NOPE)
    q_rope = jnp.dot(q_compressed, w_q_rope, preferred_element_type=jnp.float32).reshape(
        token_count, heads_here, ROPE
    )
    absorbed = jnp.einsum("thn,hnl->thl", q_nope, w_uk, preferred_element_type=jnp.float32)
    queries = (jnp.concatenate([absorbed, q_rope], axis=2) * (NOPE + ROPE) ** (-0.5)).astype(
        jnp.bfloat16
    )
    queries_seq = queries.reshape(seq_group, DRAFT, heads_here, key_width)
    draft_log, draft_mix = draft_partials(
        queries_seq, draft_kv.reshape(seq_group, DRAFT, key_width)
    )
    group_table = lax.dynamic_index_in_dim(slot_sequence, group_index, 0, keepdims=False)
    outgoing = jnp.broadcast_to(
        queries_seq.reshape(1, -1, key_width), (group_count, token_count * heads_here, key_width)
    )
    (gathered,) = exchange("group", 0, outgoing)
    back_log, back_mix = attend_slots(
        1,
        gathered.reshape(group_count * seq_group, DRAFT * heads_here, key_width),
        kv_cache[0, 0],
        context_length,
        slot_sequence,
        slot_slab,
    )
    seq_total = group_count * seq_group
    group_log, group_mix = merge_blocks(
        back_log.reshape(-1, DRAFT, heads_here),
        back_mix.reshape(-1, DRAFT, heads_here, LATENT),
        group_table.reshape(-1),
        jnp.full((seq_total, DRAFT, heads_here), EMPTY, jnp.float32),
        jnp.zeros((seq_total, DRAFT, heads_here, LATENT), jnp.float32),
    )
    home_log, home_mix = exchange_partials(
        "group",
        3,
        group_log.reshape(group_count, seq_group, DRAFT, heads_here),
        group_mix.reshape(group_count, seq_group, DRAFT, heads_here, LATENT),
    )
    home_owner = jnp.tile(jnp.arange(seq_group, dtype=jnp.int32), group_count)
    final_log, final_mix = merge_blocks(
        home_log.reshape(-1, DRAFT, heads_here),
        home_mix.reshape(-1, DRAFT, heads_here, LATENT),
        home_owner,
        draft_log,
        draft_mix,
    )
    attended = final_mix.astype(jnp.bfloat16).reshape(token_count, heads_here, LATENT)
    head_values = jnp.einsum("thl,hlv->thv", attended, w_uv, preferred_element_type=jnp.float32)
    head_values = head_values.astype(jnp.bfloat16).reshape(token_count, heads_here * VDIM)
    partial = jnp.dot(head_values, w_o, preferred_element_type=jnp.float32)
    (terms,) = exchange(
        "dev", 4, partial.reshape(holder_count, token_count // holder_count, -1)
    )
    return jnp.sum(terms, axis=0)


def solution(mesh):
    placed = (
        P("group", None),
        P(None, "dev"),
        P(None, "dev"),
        P("dev", None, None),
        P("dev", None, None),
        P("dev", None),
        P("group", "dev", None, None, None),
        P("group", None),
        P(),
        P(),
        P(),
    )
    return jax.shard_map(
        shards, mesh=mesh, in_specs=placed, out_specs=P(("group", "dev"), None), check_vma=False
    )
```

```python
import jax
import jax.numpy as jnp
from jax import lax
from jax.experimental import pallas as pl
from jax.experimental.pallas import tpu as pltpu
from jax.sharding import PartitionSpec as P

NOPE = 128
ROPE = 64
LATENT = 512
VDIM = 128
DRAFT = 4


EMPTY = -1e30


def exchange(axis, call_id, *blocks):
    count = lax.axis_size(axis)
    number = len(blocks)

    def body(*refs):
        sent, got = refs[:number], refs[number : 2 * number]
        send_sems, recv_sems, local_sems = refs[2 * number :]
        me = lax.axis_index(axis)
        barrier = pltpu.get_barrier_semaphore()
        for step in range(1, count):
            pl.semaphore_signal(
                barrier,
                inc=1,
                device_id={axis: lax.rem(me + step, count)},
                device_id_type=pl.DeviceIdType.MESH,
            )
        pl.semaphore_wait(barrier, count - 1)
        started = []
        for step in range(1, count):
            peer = lax.rem(me + step, count)
            for which in range(number):
                copy = pltpu.make_async_remote_copy(
                    src_ref=sent[which].at[peer],
                    dst_ref=got[which].at[me],
                    send_sem=send_sems.at[which, step],
                    recv_sem=recv_sems.at[which, step],
                    device_id={axis: peer},
                    device_id_type=pl.DeviceIdType.MESH,
                )
                copy.start()
                started.append(copy)
        own = []
        for which in range(number):
            copy = pltpu.make_async_copy(
                sent[which].at[me], got[which].at[me], local_sems.at[which]
            )
            copy.start()
            own.append(copy)
        for copy in own:
            copy.wait()
        for copy in started:
            copy.wait()

    vmem = pl.BlockSpec(memory_space=pltpu.VMEM)
    return pl.pallas_call(
        body,
        out_shape=tuple(jax.ShapeDtypeStruct(block.shape, block.dtype) for block in blocks),
        in_specs=[vmem] * number,
        out_specs=tuple([vmem] * number),
        scratch_shapes=[
            pltpu.SemaphoreType.DMA((number, count)),
            pltpu.SemaphoreType.DMA((number, count)),
            pltpu.SemaphoreType.DMA((number,)),
        ],
        compiler_params=pltpu.CompilerParams(
            collective_id=call_id, has_side_effects=True, vmem_limit_bytes=8 * 1024 * 1024
        ),
        name="exchange_%d" % call_id,
    )(*blocks)


def exchange_partials(axis, call_id, block_log, block_mix):
    count = lax.axis_size(axis)
    flat_log = block_log.reshape(count, 1, -1)
    width = flat_log.shape[2]
    padded = -(-width // 128) * 128
    flat_log = jnp.pad(flat_log, ((0, 0), (0, 0), (0, padded - width)))
    flat_mix = block_mix.astype(jnp.bfloat16).reshape(count, -1, block_mix.shape[-1])
    got_log, got_mix = exchange(axis, call_id, flat_log, flat_mix)
    return (
        got_log[:, :, :width].reshape(block_log.shape),
        got_mix.reshape(block_mix.shape).astype(jnp.float32),
    )


def attend_slots(call_id, every_seq, cache_slots, context_length, slot_sequence, slot_slab):
    count = lax.axis_size("dev")
    slot_count, key_width, slab_length = cache_slots.shape
    seq_total, rows, _ = every_seq.shape
    chunk = min(count, max(1, 128 // rows))
    while count % chunk:
        chunk -= 1
    steps = count // chunk
    lanes = -(-rows // 128) * 128
    log_rows = -(-slot_count // 8) * 8

    def body(
        lengths, owners, slabs, every, cache, got_log, got_mix,
        staged, arrived, keys, log_stage, mix_stage,
        key_sems, send_sems, arrive_sems, back_send, back_recv,
    ):
        group = lax.axis_index("group")
        me = lax.axis_index("dev")
        barrier = pltpu.get_barrier_semaphore()

        def greet(step, carry):
            pl.semaphore_signal(
                barrier,
                inc=1,
                device_id={"dev": lax.rem(me + step, count)},
                device_id_type=pl.DeviceIdType.MESH,
            )
            return carry

        lax.fori_loop(1, count, greet, 0)
        for slot in range(slot_count):
            pltpu.make_async_copy(cache.at[slot], keys.at[slot], key_sems.at[slot]).start()
        pl.semaphore_wait(barrier, count - 1)

        def row_copy(peer, source):
            return pltpu.make_async_remote_copy(
                src_ref=staged.at[peer],
                dst_ref=arrived.at[source],
                send_sem=send_sems.at[peer],
                recv_sem=arrive_sems.at[source],
                device_id={"dev": peer},
                device_id_type=pl.DeviceIdType.MESH,
            )

        def back_copies(peer, source):
            return [
                pltpu.make_async_remote_copy(
                    src_ref=stage.at[peer],
                    dst_ref=target.at[source],
                    send_sem=back_send.at[which, peer],
                    recv_sem=back_recv.at[which, source],
                    device_id={"dev": peer},
                    device_id_type=pl.DeviceIdType.MESH,
                )
                for which, (stage, target) in enumerate([(log_stage, got_log), (mix_stage, got_mix)])
            ]

        def send_rows(step, carry):
            peer = lax.rem(me + step, count)
            for slot in range(slot_count):
                owner = jnp.maximum(owners[group, peer, slot], 0)
                staged[peer, slot] = every[owner]
            row_copy(peer, me).start()
            return carry

        lax.fori_loop(1, count, send_rows, 0)
        limits = []
        for slot in range(slot_count):
            owner = owners[group, me, slot]
            arrived[me, slot] = every[jnp.maximum(owner, 0)]
            left = lengths[jnp.maximum(owner, 0)] - slabs[group, me, slot] * slab_length
            limits.append(jnp.where(owner >= 0, left, 0))
        for slot in range(slot_count):
            pltpu.make_async_copy(cache.at[slot], keys.at[slot], key_sems.at[slot]).wait()

        def one_step(step, carry):
            first = lax.rem(me // chunk + steps - step, steps) * chunk
            for at in range(chunk):
                source = first + at

                @pl.when(source != me)
                def _():
                    row_copy(source, source).wait_recv()

            for slot in range(slot_count):
                block = arrived[pl.ds(first, chunk), slot].reshape(chunk * rows, key_width)
                scores = lax.dot_general(
                    block, keys[slot], (((1,), (0,)), ((), ())), preferred_element_type=jnp.float32
                )
                place = lax.broadcasted_iota(jnp.int32, (1, slab_length), 1)
                is_valid = place < limits[slot]
                masked = jnp.where(is_valid, scores, EMPTY)
                peak = jnp.max(masked, axis=1, keepdims=True)
                weights = jnp.where(is_valid, jnp.exp(masked - peak), 0.0)
                total = jnp.maximum(jnp.sum(weights, axis=1, keepdims=True), 1.0)
                mixture = lax.dot_general(
                    weights.astype(jnp.bfloat16),
                    keys[slot, :LATENT],
                    (((1,), (1,)), ((), ())),
                    preferred_element_type=jnp.float32,
                )
                log = jnp.broadcast_to(peak + jnp.log(total), (chunk * rows, 128))
                mix = (mixture / total).astype(jnp.bfloat16).reshape(chunk, rows, LATENT)
                for at in range(chunk):
                    mix_stage[first + at, slot] = mix[at]
                    turned = jnp.transpose(log[at * rows : (at + 1) * rows])
                    log_stage[first + at, slot : slot + 1, :rows] = turned[:1]
            for at in range(chunk):
                source = first + at

                @pl.when(source != me)
                def _():
                    for copy in back_copies(source, me):
                        copy.start()

            return carry

        lax.fori_loop(0, steps, one_step, 0)
        got_log[me] = log_stage[me]
        got_mix[me] = mix_stage[me]

        def finish(step, carry):
            peer = lax.rem(me + step, count)
            row_copy(peer, peer).wait_send()
            for copy in back_copies(peer, peer):
                copy.wait_send()
                copy.wait_recv()
            return carry

        lax.fori_loop(1, count, finish, 0)

    smem = pl.BlockSpec(memory_space=pltpu.SMEM)
    vmem = pl.BlockSpec(memory_space=pltpu.VMEM)
    log_shape = (count, log_rows, lanes)
    mix_shape = (count, slot_count, rows, LATENT)
    got_log, got_mix = pl.pallas_call(
        body,
        out_shape=(
            jax.ShapeDtypeStruct(log_shape, jnp.float32),
            jax.ShapeDtypeStruct(mix_shape, jnp.bfloat16),
        ),
        in_specs=[smem, smem, smem, vmem, pl.BlockSpec(memory_space=pl.ANY)],
        out_specs=(vmem, vmem),
        scratch_shapes=[
            pltpu.VMEM((count, slot_count, rows, key_width), jnp.bfloat16),
            pltpu.VMEM((count, slot_count, rows, key_width), jnp.bfloat16),
            pltpu.VMEM((slot_count, key_width, slab_length), jnp.bfloat16),
            pltpu.VMEM(log_shape, jnp.float32),
            pltpu.VMEM(mix_shape, jnp.bfloat16),
            pltpu.SemaphoreType.DMA((slot_count,)),
            pltpu.SemaphoreType.DMA((count,)),
            pltpu.SemaphoreType.DMA((count,)),
            pltpu.SemaphoreType.DMA((2, count)),
            pltpu.SemaphoreType.DMA((2, count)),
        ],
        compiler_params=pltpu.CompilerParams(
            collective_id=call_id, has_side_effects=True, vmem_limit_bytes=24 * 1024 * 1024
        ),
        name="attend_slots",
    )(
        context_length,
        slot_sequence,
        slot_slab,
        every_seq,
        cache_slots,
    )
    return got_log[:, :slot_count, :rows], got_mix.astype(jnp.float32)


def merge_blocks(block_log, block_out, block_owner, own_log, own_out):
    owners_count = own_log.shape[0]
    matches = block_owner[None, :] == jnp.arange(owners_count, dtype=jnp.int32)[:, None]
    picked = jnp.where(matches[:, :, None, None], block_log[None], EMPTY)
    top_log = jnp.maximum(jnp.max(picked, axis=1), own_log)
    weights = jnp.where(matches[:, :, None, None], jnp.exp(picked - top_log[:, None]), 0.0)
    own_weight = jnp.exp(own_log - top_log)
    weight_sum = jnp.sum(weights, axis=1) + own_weight
    summed = jnp.einsum("sbtx,btxl->stxl", weights, block_out, precision=lax.Precision.HIGHEST)
    summed = summed + own_weight[..., None] * own_out
    return (top_log + jnp.log(weight_sum), summed / weight_sum[..., None])


def draft_partials(queries_seq, draft_rows):
    scores = jnp.einsum(
        "sthk,suk->sthu", queries_seq, draft_rows, preferred_element_type=jnp.float32
    )
    causal = jnp.arange(DRAFT)[None, :] <= jnp.arange(DRAFT)[:, None]
    masked = jnp.where(causal[None, :, None, :], scores, EMPTY)
    draft_peak = jnp.max(masked, axis=3)
    weights = jnp.where(causal[None, :, None, :], jnp.exp(masked - draft_peak[..., None]), 0.0)
    draft_total = jnp.sum(weights, axis=3)
    mixture = jnp.einsum(
        "sthu,sul->sthl",
        weights.astype(jnp.bfloat16),
        draft_rows[..., :LATENT],
        preferred_element_type=jnp.float32,
    )
    return (draft_peak + jnp.log(draft_total), mixture / draft_total[..., None])


def shards(
    q_compressed,
    w_q_nope,
    w_q_rope,
    w_uk,
    w_uv,
    w_o,
    kv_cache,
    draft_kv,
    context_length,
    slot_sequence,
    slot_slab,
):
    group_count = lax.axis_size("group")
    holder_count = lax.axis_size("dev")
    group_index = lax.axis_index("group")
    token_count = q_compressed.shape[0]
    seq_group = token_count // DRAFT
    heads_here = w_uk.shape[0]
    key_width = LATENT + ROPE
    q_nope = jnp.dot(q_compressed, w_q_nope, preferred_element_type=jnp.float32).astype(
        jnp.bfloat16
    )
    q_nope = q_nope.reshape(token_count, heads_here, NOPE)
    q_rope = jnp.dot(q_compressed, w_q_rope, preferred_element_type=jnp.float32).reshape(
        token_count, heads_here, ROPE
    )
    absorbed = jnp.einsum("thn,hnl->thl", q_nope, w_uk, preferred_element_type=jnp.float32)
    queries = (jnp.concatenate([absorbed, q_rope], axis=2) * (NOPE + ROPE) ** (-0.5)).astype(
        jnp.bfloat16
    )
    queries_seq = queries.reshape(seq_group, DRAFT, heads_here, key_width)
    draft_log, draft_mix = draft_partials(
        queries_seq, draft_kv.reshape(seq_group, DRAFT, key_width)
    )
    group_table = lax.dynamic_index_in_dim(slot_sequence, group_index, 0, keepdims=False)
    outgoing = jnp.broadcast_to(
        queries_seq.reshape(1, -1, key_width), (group_count, token_count * heads_here, key_width)
    )
    (gathered,) = exchange("group", 0, outgoing)
    back_log, back_mix = attend_slots(
        1,
        gathered.reshape(group_count * seq_group, DRAFT * heads_here, key_width),
        jnp.swapaxes(kv_cache[0, 0], 1, 2),
        context_length,
        slot_sequence,
        slot_slab,
    )
    seq_total = group_count * seq_group
    group_log, group_mix = merge_blocks(
        back_log.reshape(-1, DRAFT, heads_here),
        back_mix.reshape(-1, DRAFT, heads_here, LATENT),
        group_table.reshape(-1),
        jnp.full((seq_total, DRAFT, heads_here), EMPTY, jnp.float32),
        jnp.zeros((seq_total, DRAFT, heads_here, LATENT), jnp.float32),
    )
    home_log, home_mix = exchange_partials(
        "group",
        3,
        group_log.reshape(group_count, seq_group, DRAFT, heads_here),
        group_mix.reshape(group_count, seq_group, DRAFT, heads_here, LATENT),
    )
    home_owner = jnp.tile(jnp.arange(seq_group, dtype=jnp.int32), group_count)
    final_log, final_mix = merge_blocks(
        home_log.reshape(-1, DRAFT, heads_here),
        home_mix.reshape(-1, DRAFT, heads_here, LATENT),
        home_owner,
        draft_log,
        draft_mix,
    )
    attended = final_mix.astype(jnp.bfloat16).reshape(token_count, heads_here, LATENT)
    head_values = jnp.einsum("thl,hlv->thv", attended, w_uv, preferred_element_type=jnp.float32)
    head_values = head_values.astype(jnp.bfloat16).reshape(token_count, heads_here * VDIM)
    partial = jnp.dot(head_values, w_o, preferred_element_type=jnp.float32)
    (terms,) = exchange(
        "dev", 4, partial.reshape(holder_count, token_count // holder_count, -1)
    )
    return jnp.sum(terms, axis=0)


def solution(mesh):
    placed = (
        P("group", None),
        P(None, "dev"),
        P(None, "dev"),
        P("dev", None, None),
        P("dev", None, None),
        P("dev", None),
        P("group", "dev", None, None, None),
        P("group", None),
        P(),
        P(),
        P(),
    )
    return jax.shard_map(
        shards, mesh=mesh, in_specs=placed, out_specs=P(("group", "dev"), None), check_vma=False
    )
```
